128 devices in a mesh: grp: 8 (over z, core), narrow: 16 (over y, x).
Axes of the slice: x: 4, y: 4, z: 4, core: 2. Of those that a mesh axis runs over, the one named last changes fastest.
Arguments:
- panel: bfloat16 [64, 229376], P(None, ('grp', 'narrow')), may hold values from -6 to 6
- tiles: bfloat16 [65536, 128, 128], P(('grp', 'narrow')), may hold values from -0.125 to 0.125
- tile_row: int32 [65536], P(('grp', 'narrow')), may hold values from 0 to 1791, as said below
- tile_col: int32 [65536], P(('grp', 'narrow')), may hold values from 0 to 1791, as said below
- tile_count: int32 [128], P(('grp', 'narrow')), may hold values from 128 to 512, as said below
Outputs:
- filtered: bfloat16 [64, 229376], P(None, ('grp', 'narrow'))
- normal_image: float32 [64, 229376], P(None, ('grp', 'narrow'))
The draws below stay inside these ranges and needn't reach their ends.
Inputs may be any that keep to these rules, and one draw needn't show every extreme that they name: tile_row of a slot on a device of grp index g lies in g * 224 .. (g + 1) * 224 - 1. tile_col of a slot on a device of grp index g lies in (g - 1) * 224 .. (g + 1) * 224 - 1, and in g * 224 .. for g = 0. `tile_count`: some device holds 512 live slots.
All inputs are finite; a program needn't handle non-finite values.
Results may differ from the reference program's by a relative error of at most 0.009.
Values may be sent and summed in bfloat16 or wider, within the bound.
No kernel may reach another device: no remote copies, remote signals or barrier semaphores. Data moves between devices by JAX's collectives and lax.ppermute only.
A program may use at most 128 MiB of HBM per device.

```python
import jax
import jax.numpy as jnp
from jax import lax

COLS = 64
TILE = 128
NBD = 14
TILE_DEV = 512
NBG = 224
NPIX = 229376
SLOTS = 65536
N_NARROW = 16
DEVICES = 128


def slot_group(count):
    return jnp.arange(count) // TILE_DEV // N_NARROW


def draw_tile_row(key, part):
    group = slot_group(SLOTS)
    offset = jax.random.randint(jax.random.fold_in(key, 11), (SLOTS,), 0, NBG)
    return (group * NBG + offset).astype(jnp.int32)


def draw_tile_col(key, part):
    group = slot_group(SLOTS)
    offset = jax.random.randint(jax.random.fold_in(key, 23), (SLOTS,), 0, NBG)
    before = jax.random.randint(jax.random.fold_in(key, 37), (SLOTS,), 0, 2)
    before = jnp.where(group > 0, before, 0)
    return (group * NBG + offset - before * NBG).astype(jnp.int32)


def draw_tile_count(key, part):
    divisor = jax.random.randint(jax.random.fold_in(key, 41), (DEVICES,), 1, 5)
    counts = TILE_DEV // divisor
    fullest = jax.random.randint(jax.random.fold_in(key, 53), (), 0, DEVICES)
    counts = jnp.where(jnp.arange(DEVICES) == fullest, TILE_DEV, counts)
    return counts.astype(jnp.int32)


def level_of(key, dims, shards, least, top_value):
    factor_of, own = 1.0, jax.random.fold_in(key, 6)
    for position, parts in shards:
        steps = jnp.exp(jax.random.uniform(jax.random.fold_in(own, position), (parts,), jnp.float32, least / len(shards), top_value / len(shards)))
        factor_of = factor_of * jnp.repeat(steps, dims[position] // parts).reshape([-1 if axis == position else 1 for axis in range(len(dims))])
    return factor_of


def centred(stream_key, extent, spread, bound, shards=(), held_as=jnp.bfloat16):
    values = spread * jax.random.normal(stream_key, extent, jnp.float32)
    if shards:
        values = values * level_of(stream_key, extent, shards, -0.22, 0.18)
    return jnp.clip(values, -bound, bound).astype(held_as)


def setup_inputs(seed: int = 0) -> dict:
    arg_keys = jax.random.split(jax.random.key(seed), 6)
    panel = centred(arg_keys[0], (COLS, NPIX), 1.0, 6.0, ((1, 128),))
    tiles = centred(arg_keys[1], (SLOTS, TILE, TILE), (TILE * TILE_DEV // (2 * NBD)) ** -0.5, 0.125, ((0, 128),))
    tile_row = draw_tile_row(jax.random.fold_in(arg_keys[5], 71), 0)
    tile_col = draw_tile_col(jax.random.fold_in(arg_keys[5], 71), 0)
    tile_count = draw_tile_count(jax.random.fold_in(arg_keys[5], 71), 0)
    return dict(panel=panel, tiles=tiles, tile_row=tile_row, tile_col=tile_col, tile_count=tile_count)


def reference(panel, tiles, tile_row, tile_col, tile_count):
    cols = panel.shape[0]
    npix = panel.shape[1]
    nblk = npix // TILE
    slots = tiles.shape[0]
    owner = jnp.arange(slots) // TILE_DEV
    live = ((jnp.arange(slots) % TILE_DEV) < tile_count[owner]).astype(jnp.float32)
    groups = slots // TILE_DEV
    part_tiles = tiles.reshape(groups, TILE_DEV, TILE, TILE)
    rows = tile_row.reshape(groups, TILE_DEV)
    columns = tile_col.reshape(groups, TILE_DEV)
    masks = live.reshape(groups, TILE_DEV)
    blocked = panel.reshape(cols, nblk, TILE)

    def forward(acc, item):
        part, rowidx, colidx, mask = item
        pieces = blocked[:, colidx, :].astype(jnp.float32)
        prod = jnp.einsum('kti,tji->ktj', pieces, part.astype(jnp.float32)) * mask[None, :, None]
        return acc.at[:, rowidx, :].add(prod), None

    start = jnp.zeros((cols, nblk, TILE), jnp.float32)
    ysum, _ = lax.scan(forward, start, (part_tiles, rows, columns, masks))
    filtered = ysum.astype(jnp.bfloat16)

    def backward(acc, item):
        part, rowidx, colidx, mask = item
        pieces = filtered[:, rowidx, :].astype(jnp.float32)
        prod = jnp.einsum('ktj,tji->kti', pieces, part.astype(jnp.float32)) * mask[None, :, None]
        return acc.at[:, colidx, :].add(prod), None

    zsum, _ = lax.scan(backward, start, (part_tiles, rows, columns, masks))
    return filtered.reshape(cols, npix), zsum.reshape(cols, npix)
```

```python
import functools

import jax
import jax.numpy as jnp
from jax import lax
from jax.experimental import pallas as pl
from jax.experimental.pallas import tpu as pltpu
from jax.sharding import PartitionSpec as P


AXES = ("grp", "narrow")
NG, SIDE = 8, 4
NN = SIDE * SIDE
CHUNK, RING, UNROLL = 32, 6, 16
BF, F32 = jnp.bfloat16, jnp.float32


def index_of(g, y, x):
    return g * NN + y * SIDE + x


def ring_pairs(axes, step):
    pairs = []
    for g in range(NG):
        for y in range(SIDE):
            for x in range(SIDE):
                if axes[g % 2] == "y":
                    to = index_of(g, (y + step) % SIDE, x)
                else:
                    to = index_of(g, y, (x + step) % SIDE)
                pairs.append((index_of(g, y, x), to))
    return pairs


def group_pairs(moves):
    return [(s * NN + n, d * NN + n) for s, d in moves for n in range(NN)]


def permute(value, pairs):
    return lax.ppermute(value, AXES, pairs)


def small(value, step):
    return permute(value, ring_pairs("xy", step))


def big(value, step):
    return permute(value, ring_pairs("yx", step))


def swap(value):
    return permute(value, group_pairs([(g, g ^ 1) for g in range(NG)]))


def gather(mine):
    n = mine.shape[0]
    h, half = n // 2, 2 * n
    minus, plus = small(mine, 1), small(mine, -1)
    far0, far1 = small(minus[:h], 1), small(plus[h:], -1)
    line = jnp.concatenate([mine, minus, plus, far0, far1], 0)
    m0 = big(line[:half], 1)
    p1 = big(line[half:], -1)
    m1 = big(line[half:], 1)
    p0 = big(line[:half], -1)
    o0, o1 = big(m0, 1), big(p1, -1)
    return [line, m0, m1, p0, p1, o0, o1]


def scatter_line(move, own, m0, m1, p0, p1, o0, o1):
    from_m, from_p = move(o0, 1), move(o1, -1)
    s1, s0 = move(p1, 1), move(m0, -1)
    t0 = move((p0.astype(F32) + from_m.astype(F32)).astype(BF), 1)
    t1 = move((m1.astype(F32) + from_p.astype(F32)).astype(BF), -1)
    k = t0.shape[0]
    lo = own[:k].astype(F32) + s0.astype(F32) + t0.astype(F32)
    hi = own[k:].astype(F32) + s1.astype(F32) + t1.astype(F32)
    return jnp.concatenate([lo, hi], 0)


def scatter_small(parts):
    h = parts[0].shape[0] // 2
    m, p, o = (v.astype(BF) for v in parts[1:])
    return scatter_line(small, parts[0], m[:h], m[h:], p[:h], p[h:], o[:h], o[h:])


def load_tiles(tiles, buf, sem, c):
    slot = lax.rem(c, RING)
    return pltpu.make_async_copy(tiles.at[pl.ds(c * CHUNK, CHUNK)], buf.at[slot], sem.at[slot])


def product_loop(chunks, contract, src, dst, tiles, buf, tsem, held, acc):
    def chunk(c, carry):
        load_tiles(tiles, buf, tsem, c).wait()
        slot = lax.rem(c, RING)

        def turn(s, carry):
            prods, rows = [], []
            for u in range(UNROLL):
                k = s * UNROLL + u
                t = c * CHUNK + k
                prods.append(
                    lax.dot_general(
                        held[src[t]],
                        buf[slot, k],
                        (((1,), (contract,)), ((), ())),
                        preferred_element_type=F32,
                    )
                )
                rows.append(dst[t])
            for u in range(UNROLL):
                acc[rows[u]] += prods[u]
            return carry

        lax.fori_loop(0, CHUNK // UNROLL, turn, 0)

        @pl.when(c + RING < chunks)
        def _():
            load_tiles(tiles, buf, tsem, c + RING).start()

        return carry

    lax.fori_loop(0, chunks, chunk, 0)


def kernel(n_in, contract, outs, count, src, dst, tiles, *refs):
    sources, refs = refs[:n_in], refs[n_in:]
    results, refs = refs[: len(outs)], refs[len(outs) :]
    buf, held, acc, tsem, hsem, osem = refs[:6]
    stages = refs[6:]
    chunks = (count[0] + CHUNK - 1) // CHUNK

    def first(c, carry):
        load_tiles(tiles, buf, tsem, c).start()
        return carry

    copies, at = [], 0
    for i, ref in enumerate(sources):
        n = ref.shape[0]
        copies.append(pltpu.make_async_copy(ref, held.at[pl.ds(at, n)], hsem.at[i]))
        copies[-1].start()
        at += n
    lax.fori_loop(0, jnp.minimum(chunks, RING), first, 0)
    acc[...] = jnp.zeros_like(acc)
    for copy in copies:
        copy.wait()
    product_loop(chunks, contract, src, dst, tiles, buf, tsem, held, acc)
    copies = []
    for i, (start, n, dtype) in enumerate(outs):
        stages[i][...] = acc[pl.ds(start, n)].astype(dtype)
        copies.append(pltpu.make_async_copy(stages[i], results[i], osem.at[i]))
        copies[-1].start()
    for copy in copies:
        copy.wait()


def products(name, contract, outs, blocks, count, src, dst, tiles, sources):
    cols, tile = sources[0].shape[1:]
    held = sum(s.shape[0] for s in sources)
    any_space = pl.BlockSpec(memory_space=pl.ANY)
    shapes = [(n, cols, tile) for _, n, _ in outs]
    return pl.pallas_call(
        functools.partial(kernel, len(sources), contract, outs),
        out_shape=[jax.ShapeDtypeStruct(s, o[2]) for s, o in zip(shapes, outs)],
        in_specs=[pl.BlockSpec(memory_space=pltpu.SMEM)] * 3 + [any_space] * (1 + len(sources)),
        out_specs=[any_space] * len(outs),
        scratch_shapes=[
            pltpu.VMEM((RING, CHUNK, tile, tile), BF),
            pltpu.VMEM((held, cols, tile), BF),
            pltpu.VMEM((blocks + 1, cols, tile), F32),
            pltpu.SemaphoreType.DMA((RING,)),
            pltpu.SemaphoreType.DMA((len(sources),)),
            pltpu.SemaphoreType.DMA((len(outs),)),
        ]
        + [pltpu.VMEM(s, o[2]) for s, o in zip(shapes, outs)],
        compiler_params=pltpu.CompilerParams(vmem_limit_bytes=36 << 20),
        cost_estimate=pl.CostEstimate(
            flops=2 * tiles.shape[0] * cols * tile * tile,
            bytes_accessed=tiles.size * 2,
            transcendentals=0,
        ),
        name=name,
    )(count, src, dst, tiles, *sources)


def body(panel, tiles, tile_row, tile_col, tile_count):
    cols, width = panel.shape
    slots, tile = tiles.shape[:2]
    nbd = width // tile
    nbg = nbd * NN
    sub = nbd // 2
    wide = nbd + sub
    group, place = lax.axis_index("grp"), lax.axis_index("narrow")
    core = group % 2
    y, x = place // SIDE, place % SIDE

    def ring_slot(delta):
        d = delta % SIDE
        return jnp.where(d == 0, 0, jnp.where(d == SIDE - 1, 1, jnp.where(d == 1, 2, 3)))

    def locate(block):
        owner, b = block // nbd, block % nbd
        sy, sx = ring_slot(owner // SIDE - y), ring_slot(owner % SIDE - x)
        yx, xy = sy * SIDE + sx, sx * SIDE + sy
        return jnp.where(core == 0, yx, xy), jnp.where(core == 0, xy, yx), b

    live = jnp.arange(slots) < tile_count[0]
    here, _, b = locate(tile_row - group * nbg)
    row_at = here * nbd + b
    col = tile_col - (group - 1) * nbg
    own = col >= nbg
    here, there, b = locate(jnp.where(own, col - nbg, col))
    low = b < sub
    nh, nw = NN * sub, NN * wide
    fsrc = jnp.where(
        own,
        here * wide + b,
        jnp.where(
            core == 1,
            nw + there * wide + b,
            jnp.where(low, here * wide + nbd + b, nw + there * wide + wide - nbd + b),
        ),
    )
    bdst = jnp.where(
        own,
        here * nbd + b,
        jnp.where(
            core == 1,
            nbg + jnp.where(low, there * sub + b, nh + there * sub + b - sub),
            nbg + jnp.where(low, nh + here * sub + b, there * sub + b - sub),
        ),
    )
    fdst = jnp.where(live, row_at, nbg)
    bdst = jnp.where(live, bdst, 2 * nbg)

    mine = panel.reshape(cols, nbd, tile).transpose(1, 0, 2)
    odd = range(1, NG - 1, 2)
    prior = permute(mine[:sub], group_pairs([(g, g + 1) for g in odd])) + permute(
        mine[sub:], group_pairs([(g, g + 2) for g in odd])
    )
    held = gather(jnp.concatenate([mine, prior], 0))
    other = [swap(v) for v in held]

    line = SIDE * nbd
    hl = line // 2
    outs = [(0, line, F32)] + [(line + i * hl, hl, BF) for i in range(6)]
    parts = products("rows", 1, outs, nbg, tile_count, fsrc, fdst, tiles, held + other)
    mid = scatter_line(big, *parts)
    mine = scatter_small([mid[i * nbd : (i + 1) * nbd] for i in range(SIDE)])
    filtered = mine.astype(BF)

    held = gather(filtered)
    outs = [(0, nbg, BF), (nbg, nh, BF), (nbg + nh, nh, BF)]
    sums, send0, send1 = products("columns", 0, outs, 2 * nbg, tile_count, row_at, bdst, tiles, held)
    got0 = swap(send0)
    got1 = permute(send1, group_pairs([(g, g - 1) for g in range(1, NG, 2)]))
    first = core == 0
    k = SIDE * sub
    units = []
    for s in range(SIDE):
        own_part = sums[s * line : (s + 1) * line].reshape(SIDE, nbd, cols, tile).astype(F32)
        g0 = got0[s * k : (s + 1) * k].astype(F32)
        g1 = got1[s * k : (s + 1) * k].reshape(SIDE, sub, cols, tile).astype(F32)
        extra = jnp.concatenate([jnp.where(first, g0, 0).reshape(SIDE, sub, cols, tile), g1], 1)
        prior_part = jnp.where(first, send1[s * k : (s + 1) * k].astype(F32), g0)
        units.append(
            jnp.concatenate([(own_part + extra).reshape(line, cols, tile), prior_part], 0)
        )
    unit = line + k
    hu = unit // 2
    m, p, o = (v.astype(BF) for v in units[1:])
    mid = scatter_line(big, units[0], m[:hu], m[hu:], p[:hu], p[hu:], o[:hu], o[hu:])
    mid = scatter_small(
        [
            jnp.concatenate(
                [mid[i * nbd : (i + 1) * nbd], mid[line + i * sub : line + (i + 1) * sub]], 0
            )
            for i in range(SIDE)
        ]
    )
    back = mid[nbd:].astype(BF)
    from_next = jnp.concatenate(
        [
            permute(back, group_pairs([(g + 1, g) for g in odd])),
            permute(back, group_pairs([(g + 2, g) for g in odd])),
        ],
        0,
    )
    result = mid[:nbd] + from_next.astype(F32)

    def flat(v):
        return v.transpose(1, 0, 2).reshape(cols, width)

    return (flat(filtered), flat(result))


def solution(mesh):
    placed = (
        P(None, AXES),
        P(AXES, None, None),
        P(AXES),
        P(AXES),
        P(AXES),
    )
    return jax.shard_map(
        body,
        mesh=mesh,
        in_specs=placed,
        out_specs=(P(None, AXES), P(None, AXES)),
        check_vma=False,
    )
```
